512 devices in a mesh: row: 32 (over y_hi, x, core), col: 16 (over z, y_lo).
Axes of the slice: x: 4, y: 8 (y_hi: 4, y_lo: 2; y = y_hi * 2 + y_lo), z: 8, core: 2. Of those that a mesh axis runs over, the one named last changes fastest.
Arguments:
- density: float32 [4096, 4096], P('row', 'col'), may hold values from -1 to 1, as said below
- pattern: int32 [32, 32], P('row', 'col'), may hold values from 0 to 1, as said below
- step_choices: int32 [2], replicated, may hold values from 0 to 1, as said below
Outputs:
- purified: float32 [4096, 4096], P('row', 'col')
- traces: float32 [2], replicated
The draws below stay inside these ranges and needn't reach their ends.
Inputs may be any that keep to these rules, and one draw needn't show every extreme that they name: `pattern`: symmetric; every diagonal block is 1. `density`: symmetric, and zero in every block where pattern is 0. `step_choices`: one step squares and the other takes 2X - X^2.
All inputs are finite; a program needn't handle non-finite values.
Results may differ from the reference program's by a relative error of at most 0.0003.
Values sent between devices are 32-bit elements; how exact they have to be, the bound alone decides.
A program may use at most 64 MiB of HBM per device.

```python
import math
import jax
import jax.numpy as jnp
from jax import lax

B = 128
STEPS = 2
NBLK = 32
ORDER = 4096


def block_pattern(key):
    sub_key = jax.random.fold_in(key, 11)
    scores = jax.random.randint(sub_key, (NBLK, NBLK), 0, 1000)
    left = jnp.arange(NBLK)[:, None]
    right = jnp.arange(NBLK)[None, :]
    scores = jnp.where(left <= right, scores, scores.T)
    thresh = 150 + 450 * (left + right) // (2 * max(NBLK - 1, 1))
    live = (scores < thresh) | (left == right)
    return live.astype(jnp.int32)


def draw_pattern(key, part):
    return block_pattern(key)


def draw_density(key, part):
    blocks = block_pattern(key).astype(jnp.float32)
    element_mask = jnp.repeat(jnp.repeat(blocks, B, 0), B, 1)
    sub_key = jax.random.fold_in(key, 23)
    values = jax.random.truncated_normal(sub_key, -4.0, 4.0, (ORDER, ORDER), jnp.float32)
    index_line = jnp.arange(ORDER)
    values = jnp.where(index_line[:, None] <= index_line[None, :], values, values.T)
    sigma = 1.0 / math.sqrt(ORDER)
    return element_mask * values * sigma + 0.5 * jnp.eye(ORDER, dtype=jnp.float32)


def draw_step_choices(key, part):
    sub_key = jax.random.fold_in(key, 37)
    first = jax.random.randint(sub_key, (), 0, 2)
    positions = jnp.arange(STEPS, dtype=jnp.int32)
    return ((positions + first) % 2).astype(jnp.int32)


def setup_inputs(seed: int = 0) -> dict:
    arg_keys = jax.random.split(jax.random.key(seed), 4)
    return {
        "density": draw_density(jax.random.fold_in(arg_keys[3], 71), 0),
        "pattern": draw_pattern(jax.random.fold_in(arg_keys[3], 71), 0),
        "step_choices": draw_step_choices(jax.random.fold_in(arg_keys[3], 71), 0),
    }


def reference(density, pattern, step_choices):
    element_mask = jnp.repeat(jnp.repeat(pattern, B, 0), B, 1).astype(jnp.float32)
    traces = []
    for section_index in range(STEPS):
        weight = step_choices[section_index].astype(jnp.float32)
        product = jnp.dot(density, density, precision=lax.Precision.HIGHEST, preferred_element_type=jnp.float32)
        density = element_mask * ((1.0 - 2.0 * weight) * product + 2.0 * weight * density)
        traces.append(jnp.trace(density))
    return density, jnp.stack(traces)
```

```python
import heapq

import jax
import jax.numpy as jnp
from jax import lax
from jax.experimental import pallas as pl
from jax.experimental.pallas import tpu as pltpu
from jax.sharding import PartitionSpec as P

B = 128
STEPS = 2
NZ, NL, NH, NX = 8, 2, 4, 4
NK = NZ * NL
NP = 2
CROSS = (0, 2, 6)
MESH = pl.DeviceIdType.MESH
F32 = jnp.float32


def row_route(d, s, p):
    low = p < NP // 2
    go = []
    if s == 0:
        if d == 0:
            go += ["zp", "zm"]
        elif d in (1, 2) or (d == 3 and low):
            go += ["zp"]
        elif d in (7, 6) or (d == 5 and not low):
            go += ["zm"]
        if d in CROSS:
            go += ["yc"]
    else:
        if d == 0:
            go += ["zp", "zm"]
        else:
            nxt, prv = (d + 1) % NZ, (d - 1) % NZ
            if d < 4 and nxt not in CROSS and (d < 3 or low):
                go += ["zp"]
            if d > 4 and prv not in CROSS and (d > 5 or not low):
                go += ["zm"]
    return go


def col_route(e, g, p):
    low = p < NP // 2
    go = []
    if g == 0:
        if e == 0:
            go += ["yp", "ym"]
        elif e == 1 and low:
            go += ["yp"]
        elif e == 3 and not low:
            go += ["ym"]
        go += ["xp", "xm"]
    elif g == 1 and low:
        go += ["xp"]
    elif g == 3 and not low:
        go += ["xm"]
    return go


def landing(kind, i, j, way):
    if kind == "a":
        if way == "yc":
            return i, 1 - j
        return ((i + (1 if way == "zp" else -1)) % NZ, j)
    if way[0] == "y":
        return ((i + (1 if way == "yp" else -1)) % NH, j)
    return (i, (j + (1 if way == "xp" else -1)) % NX)


def arrival_order():
    wire = 2.8 / NP
    cost = {"zp": wire, "zm": wire, "yc": wire, "xp": wire, "xm": wire, "yp": 2 * wire, "ym": 2 * wire}
    lag = {"zp": 1.7, "zm": 1.7, "yc": 1.7, "xp": 1.7, "xm": 1.7, "yp": 2.4, "ym": 2.4}
    free = dict.fromkeys(cost, 0.0)
    ready, order, tick = [], [], 0
    for p in range(NP):
        heapq.heappush(ready, (0.0, tick, ("b", 0, 0, p)))
        heapq.heappush(ready, (1.0 * (p >= NP // 2), tick + 1, ("a", 0, 0, p)))
        tick += 2
    while ready:
        now, _, (kind, i, j, p) = heapq.heappop(ready)
        if (i, j) != (0, 0):
            order.append((kind, i, j, p))
        for way in (row_route if kind == "a" else col_route)(i, j, p):
            start = max(now, free[way])
            free[way] = start + cost[way]
            ii, jj = landing(kind, i, j, way)
            heapq.heappush(ready, (free[way] + lag[way], tick, (kind, ii, jj, p)))
            tick += 1
    return order


ORDER = arrival_order()
assert len(ORDER) == len(set(ORDER)) == 2 * (NK - 1) * NP
NSEND = 160


def split(v):
    hi = v.astype(jnp.bfloat16)
    return hi, (v - hi.astype(F32)).astype(jnp.bfloat16)


def fold(v):
    return jnp.sum(v.reshape(-1, 8, 2, 128), axis=(0, 2))


def kernel(choice_ref, pat_ref, x_ref, out_ref, tr_ref, abuf, bbuf, part, gift, sums, got,
           asem, bsem, swap_sem, gift_sem, tr_sem, send_sem, tr_send):
    row, col = lax.axis_index("row"), lax.axis_index("col")
    core, x, yh = row % 2, (row // 2) % NX, row // (2 * NX)
    yl, z = col % NL, col // NL

    def at(core_=None, x_=None, yh_=None, yl_=None, z_=None):
        c = core if core_ is None else core_
        xx = x if x_ is None else x_
        h = yh if yh_ is None else yh_
        l = yl if yl_ is None else yl_
        zz = z if z_ is None else z_
        return ((h * NX + xx) * 2 + c, zz * NL + l)

    near = {
        "zp": at(z_=(z + 1) % NZ),
        "zm": at(z_=(z + NZ - 1) % NZ),
        "yc": at(yl_=1 - yl),
        "yp": at(yh_=(yh + 1) % NH),
        "ym": at(yh_=(yh + NH - 1) % NH),
        "xp": at(x_=(x + 1) % NX),
        "xm": at(x_=(x + NX - 1) % NX),
        "c": at(core_=1 - core),
    }
    barrier = pltpu.get_barrier_semaphore()
    for place in near.values():
        pl.semaphore_signal(barrier, inc=1, device_id=place, device_id_type=MESH)
    pl.semaphore_wait(barrier, len(near))

    def akey(d, s):
        return ((z + NZ - d) % NZ) * NL + (yl if s == 0 else 1 - yl)

    def bkey(e, g):
        return ((yh + NH - e) % NH) * NX + (x + NX - g) % NX

    AR, BR = 2 * B // NP, B // NP

    def place(kind, step, i, j, p):
        if kind == "a":
            return abuf.at[step, akey(i, j), pl.ds(p * AR, AR), :]
        return bbuf.at[step, bkey(i, j), pl.ds(p * BR, BR), :]

    def sem_of(kind, step, i, j, p):
        return asem.at[step, i, j, p] if kind == "a" else bsem.at[step, i, j, p]

    pending = []

    def send(src, dst, step, recv_sem, where):
        copy = pltpu.make_async_remote_copy(
            src_ref=src, dst_ref=dst, send_sem=send_sem.at[step, len(pending)], recv_sem=recv_sem,
            device_id=where, device_id_type=MESH)
        copy.start()
        pending.append(copy)

    def arrive(ref, sem, step):
        pltpu.make_async_remote_copy(
            src_ref=ref, dst_ref=ref, send_sem=send_sem.at[step, NSEND - 1], recv_sem=sem,
            device_id=near["c"], device_id_type=MESH).wait_recv()

    def forward(kind, step, i, j, p, p_route, src=None):
        here = place(kind, step, i, j, p)
        for way in (row_route if kind == "a" else col_route)(i, j, p_route):
            ii, jj = landing(kind, i, j, way)
            send(here if src is None else src, here, step, sem_of(kind, step, ii, jj, p), near[way])

    mine = pl.ds(core * B, B)
    theirs = pl.ds((1 - core) * B, B)
    off = row * B - col * 2 * B
    diag = (lax.broadcasted_iota(jnp.int32, (B, 2 * B), 0) + off
            == lax.broadcasted_iota(jnp.int32, (B, 2 * B), 1)).astype(F32)
    mask = [pat_ref[0, h].astype(F32) for h in range(2)]

    groups = [
        [at(z_=(z + i) % NZ) for i in range(1, NZ)],
        [at(x_=(x + i) % NX) for i in range(1, NX)],
        [at(yh_=(yh + i) % NH) for i in range(1, NH)],
        [at(yl_=1 - yl)],
        [at(core_=1 - core)],
    ]
    tr_copies = []

    def tr_start(stage):
        for n, where in enumerate(groups[stage]):
            copy = pltpu.make_async_remote_copy(
                src_ref=sums.at[stage], dst_ref=got.at[stage, n], send_sem=tr_send.at[stage, n],
                recv_sem=tr_sem.at[stage, n], device_id=where, device_id_type=MESH)
            copy.start()
            tr_copies.append((stage, copy))

    def tr_finish(stage):
        total = sums[stage]
        for n, (_, copy) in enumerate([c for c in tr_copies if c[0] == stage]):
            copy.wait_recv()
            total = total + got[stage, n]
        sums[stage + 1] = total

    for step in range(STEPS):
        own_b = bbuf.at[step, bkey(0, 0)]
        tile = x_ref if step == 0 else own_b
        send(tile.at[:, theirs], abuf.at[step, akey(0, 0), mine, :], step, swap_sem.at[step], near["c"])
        for p in range(NP):
            forward("b", step, 0, 0, p, p, tile.at[pl.ds(p * BR, BR), :])
        now = tile[...]
        if step == 0:
            own_b[...] = now
        abuf[step, akey(0, 0), mine, :] = tile[:, mine]
        for p in range(NP // 2):
            forward("a", step, 0, 0, core * (NP // 2) + p, 0)
        arrive(abuf.at[step, akey(0, 0), theirs, :], swap_sem.at[step], step)
        for p in range(NP // 2):
            forward("a", step, 0, 0, (1 - core) * (NP // 2) + p, 0)
        sums[0, 2 * step] = fold(now * now)
        sums[0, 2 * step + 1] = fold(now * diag)
        if step == 1:
            tr_start(0)
        stage_at = {len(ORDER) * (n + 3) // 8: n for n in range(5)}
        for n, (kind, i, j, p) in enumerate(ORDER):
            arrive(place(kind, step, i, j, p), sem_of(kind, step, i, j, p), step)
            forward(kind, step, i, j, p, p)
            if step == 1 and n in stage_at:
                tr_finish(stage_at[n])
                if stage_at[n] < 4:
                    tr_start(stage_at[n] + 1)
        acc = jnp.zeros((2 * B, 2 * B), F32)
        for k in range(NK // 2):
            a = jnp.concatenate([abuf[step, 2 * k], abuf[step, 2 * k + 1]], axis=1)
            b = jnp.concatenate([bbuf[step, 2 * k], bbuf[step, 2 * k + 1]], axis=0)
            ah, al = split(a)
            bh, bl = split(b)
            acc += (jnp.dot(ah, bh, preferred_element_type=F32) + jnp.dot(al, bh, preferred_element_type=F32)
                    + jnp.dot(ah, bl, preferred_element_type=F32))
        part[step] = acc
        send(part.at[step, theirs, :], gift.at[step], step, gift_sem.at[step], near["c"])
        arrive(gift.at[step], gift_sem.at[step], step)
        product = part[step, mine, :] + gift[step]
        w = choice_ref[step].astype(F32)
        for h in range(2):
            lanes = slice(h * B, (h + 1) * B)
            new = mask[h] * ((1.0 - 2.0 * w) * product[:, lanes] + 2.0 * w * now[:, lanes])
            if step == STEPS - 1:
                out_ref[:, lanes] = new
            else:
                bbuf[step + 1, bkey(0, 0), :, lanes] = new
        for copy in pending:
            copy.wait_send()
        pending.clear()
    for _, copy in tr_copies:
        copy.wait_send()
    for step in range(STEPS):
        w = choice_ref[step].astype(F32)
        square, plain = jnp.sum(sums[5, 2 * step]), jnp.sum(sums[5, 2 * step + 1])
        tr_ref[step] = (1.0 - 2.0 * w) * square + 2.0 * w * plain


def shards(density, pattern, step_choices):
    vmem, smem = (pl.BlockSpec(memory_space=m) for m in (pltpu.VMEM, pltpu.SMEM))
    dma = pltpu.SemaphoreType.DMA
    return pl.pallas_call(
        kernel,
        out_shape=(jax.ShapeDtypeStruct(density.shape, F32), jax.ShapeDtypeStruct((STEPS,), F32)),
        in_specs=[smem, smem, vmem],
        out_specs=(vmem, smem),
        scratch_shapes=[
            pltpu.VMEM((STEPS, NK, 2 * B, B), F32),
            pltpu.VMEM((STEPS, NK, B, 2 * B), F32),
            pltpu.VMEM((STEPS, 2 * B, 2 * B), F32),
            pltpu.VMEM((STEPS, B, 2 * B), F32),
            pltpu.VMEM((6, 2 * STEPS, 8, 128), F32),
            pltpu.VMEM((5, 7, 2 * STEPS, 8, 128), F32),
            dma((STEPS, NZ, NL, NP)),
            dma((STEPS, NH, NX, NP)),
            dma((STEPS,)),
            dma((STEPS,)),
            dma((5, 7)),
            dma((STEPS, NSEND)),
            dma((5, 7)),
        ],
        compiler_params=pltpu.CompilerParams(collective_id=0, has_side_effects=True),
    )(step_choices, pattern, density)


def solution(mesh):
    return jax.shard_map(
        shards,
        mesh=mesh,
        in_specs=(P("row", "col"), P("row", "col"), P()),
        out_specs=(P("row", "col"), P()),
        check_vma=False,
    )
```

```python
import jax
import jax.numpy as jnp
from jax import lax
from jax.experimental import pallas as pl
from jax.experimental.pallas import tpu as pltpu
from jax.sharding import PartitionSpec as P

B = 128
STEPS = 2
NZ, NL, NH, NX = 8, 2, 4, 4
NK = NZ * NL
NP = 2
CROSS = (0, 3, 5)
MESH = pl.DeviceIdType.MESH
F32 = jnp.float32


def row_route(d, s, p):
    low = p < NP // 2
    go = []
    if s == 0:
        if d == 0:
            go += ["zp", "zm"]
        elif d in (1, 2) or (d == 3 and low):
            go += ["zp"]
        elif d in (7, 6) or (d == 5 and not low):
            go += ["zm"]
        if d in CROSS:
            go += ["yc"]
    else:
        if d == 0:
            go += ["zp", "zm"]
        else:
            nxt, prv = (d + 1) % NZ, (d - 1) % NZ
            if d < 4 and nxt not in CROSS and (d < 3 or low):
                go += ["zp"]
            if d > 4 and prv not in CROSS and (d > 5 or not low):
                go += ["zm"]
    return go


def col_route(e, g, p):
    low = p < NP // 2
    go = []
    if g == 0:
        if e == 0:
            go += ["yp", "ym"]
        elif e == 1 and low:
            go += ["yp"]
        elif e == 3 and not low:
            go += ["ym"]
        go += ["xp", "xm"]
    elif g == 1 and low:
        go += ["xp"]
    elif g == 3 and not low:
        go += ["xm"]
    return go


def landing(kind, i, j, way):
    if kind == "a":
        if way == "yc":
            return i, 1 - j
        return ((i + (1 if way == "zp" else -1)) % NZ, j)
    if way[0] == "y":
        return ((i + (1 if way == "yp" else -1)) % NH, j)
    return (i, (j + (1 if way == "xp" else -1)) % NX)


ORDER = [
    ("b", 0, 3, 0), ("a", 7, 0, 0), ("a", 1, 0, 0), ("b", 0, 1, 0), ("a", 7, 0, 1), ("b", 1, 0, 0),
    ("a", 1, 0, 1), ("b", 3, 0, 0), ("a", 2, 0, 0), ("b", 3, 0, 1), ("b", 1, 0, 1), ("a", 6, 0, 0),
    ("b", 0, 1, 1), ("a", 6, 0, 1), ("a", 2, 0, 1), ("a", 0, 1, 0), ("a", 0, 1, 1), ("b", 1, 1, 0),
    ("b", 0, 3, 1), ("a", 3, 0, 0), ("b", 3, 1, 0), ("b", 1, 3, 0), ("b", 2, 0, 0), ("a", 5, 0, 1),
    ("b", 2, 0, 1), ("b", 3, 3, 1), ("a", 5, 0, 0), ("a", 3, 0, 1), ("b", 1, 3, 1), ("a", 7, 1, 0),
    ("a", 1, 1, 0), ("b", 3, 3, 0), ("a", 3, 1, 0), ("a", 7, 1, 1), ("b", 1, 2, 0), ("b", 3, 2, 0),
    ("a", 1, 1, 1), ("b", 3, 1, 1), ("a", 5, 1, 1), ("b", 2, 1, 0), ("a", 4, 0, 0), ("b", 2, 3, 0),
    ("b", 0, 2, 1), ("b", 2, 3, 1), ("a", 6, 1, 0), ("a", 2, 1, 0), ("a", 4, 0, 1), ("b", 1, 1, 1),
    ("a", 6, 1, 1), ("a", 5, 1, 0), ("a", 3, 1, 1), ("a", 4, 1, 0), ("a", 2, 1, 1), ("b", 1, 2, 1),
    ("a", 4, 1, 1), ("b", 2, 1, 1), ("b", 0, 2, 0), ("b", 2, 2, 0), ("b", 3, 2, 1), ("b", 2, 2, 1),
]
assert len(ORDER) == len(set(ORDER)) == 2 * (NK - 1) * NP
STAGE_AT = {9: 0, 29: 1, 54: 2}
NSEND = 80 * NP


def split(v):
    hi = v.astype(jnp.bfloat16)
    return hi, (v - hi.astype(F32)).astype(jnp.bfloat16)


def fold(v):
    rows = jnp.sum(v, axis=0, keepdims=True)
    return rows[:, :128] + rows[:, 128:]


def kernel(choice_ref, pat_ref, x_ref, out_ref, tr_ref, abuf, bbuf, part, gift, sums, got,
           asem, bsem, swap_sem, gift_sem, tr_sem, send_sem, tr_send, fetch_sem):
    row, col = lax.axis_index("row"), lax.axis_index("col")
    core, x, yh = row % 2, (row // 2) % NX, row // (2 * NX)
    yl, z = col % NL, col // NL

    def at(core_=None, x_=None, yh_=None, yl_=None, z_=None):
        c = core if core_ is None else core_
        xx = x if x_ is None else x_
        h = yh if yh_ is None else yh_
        l = yl if yl_ is None else yl_
        zz = z if z_ is None else z_
        return ((h * NX + xx) * 2 + c, zz * NL + l)

    near = {
        "zp": at(z_=(z + 1) % NZ),
        "zm": at(z_=(z + NZ - 1) % NZ),
        "yc": at(yl_=1 - yl),
        "yp": at(yh_=(yh + 1) % NH),
        "ym": at(yh_=(yh + NH - 1) % NH),
        "xp": at(x_=(x + 1) % NX),
        "xm": at(x_=(x + NX - 1) % NX),
        "c": at(core_=1 - core),
    }
    near_other = {
        "zp": at(core_=1 - core, z_=(z + 1) % NZ),
        "zm": at(core_=1 - core, z_=(z + NZ - 1) % NZ),
        "yc": at(core_=1 - core, yl_=1 - yl),
    }
    def akey(d, s):
        return ((z + NZ - d) % NZ) * NL + (yl if s == 0 else 1 - yl)

    def bkey(e, g):
        return ((yh + NH - e) % NH) * NX + (x + NX - g) % NX

    barrier = pltpu.get_barrier_semaphore()
    greeted = [*near.values(), *near_other.values()]
    for place in greeted:
        pl.semaphore_signal(barrier, inc=1, device_id=place, device_id_type=MESH)
    sums[0] = jnp.zeros((8, 128), F32)
    fetch = pltpu.make_async_copy(x_ref, bbuf.at[0, bkey(0, 0)], fetch_sem)
    fetch.start()
    pl.semaphore_wait(barrier, len(greeted))
    fetch.wait()

    AR, BR = 2 * B // NP, B // NP

    def place(kind, step, i, j, p):
        if kind == "a":
            return abuf.at[step, akey(i, j), pl.ds(p * AR, AR), :]
        return bbuf.at[step, bkey(i, j), pl.ds(p * BR, BR), :]

    def sem_of(kind, step, i, j, p):
        return asem.at[step, i, j, p] if kind == "a" else bsem.at[step, i, j, p]

    pending = []

    def send(src, dst, step, recv_sem, where):
        copy = pltpu.make_async_remote_copy(
            src_ref=src, dst_ref=dst, send_sem=send_sem.at[step, len(pending)], recv_sem=recv_sem,
            device_id=where, device_id_type=MESH)
        copy.start()
        pending.append(copy)

    def arrive(ref, sem, step):
        pltpu.make_async_remote_copy(
            src_ref=ref, dst_ref=ref, send_sem=send_sem.at[step, NSEND - 1], recv_sem=sem,
            device_id=near["c"], device_id_type=MESH).wait_recv()

    def forward(kind, step, i, j, p, p_route):
        here = place(kind, step, i, j, p)
        for way in (row_route if kind == "a" else col_route)(i, j, p_route):
            ii, jj = landing(kind, i, j, way)
            send(here, here, step, sem_of(kind, step, ii, jj, p), near[way])

    mine = pl.ds(core * B, B)
    theirs = pl.ds((1 - core) * B, B)
    off = row * B - col * 2 * B
    diag = (lax.broadcasted_iota(jnp.int32, (B, 2 * B), 0) + off
            == lax.broadcasted_iota(jnp.int32, (B, 2 * B), 1)).astype(F32)
    mask = [pat_ref[0, h].astype(F32) for h in range(2)]

    groups = [
        [at(z_=(z + i) % NZ) for i in range(1, NZ)],
        [at(x_=(x + i) % NX, yl_=(yl + j) % NL) for i in range(NX) for j in range(NL) if i or j],
        [at(yh_=(yh + i) % NH) for i in range(1, NH)],
        [near["c"]],
    ]
    tr_copies = []

    def tr_start(stage):
        for n, where in enumerate(groups[stage]):
            copy = pltpu.make_async_remote_copy(
                src_ref=sums.at[stage], dst_ref=got.at[stage, n], send_sem=tr_send.at[stage, n],
                recv_sem=tr_sem.at[stage, n], device_id=where, device_id_type=MESH)
            copy.start()
            tr_copies.append((stage, copy))

    def tr_finish(stage):
        total = sums[stage]
        for n, (_, copy) in enumerate([c for c in tr_copies if c[0] == stage]):
            copy.wait_recv()
            total = total + got[stage, n]
        sums[stage + 1] = total

    for step in range(STEPS):
        tile = bbuf.at[step, bkey(0, 0)]
        own_a = abuf.at[step, akey(0, 0), mine, :]
        for n in range(3):
            if n < 2:
                for way in row_route(0, 0, 0)[2 * n: 2 * n + 2]:
                    landed = asem.at[step, *landing("a", 0, 0, way), core]
                    send(tile.at[:, mine], own_a, step, landed, near[way])
                    send(tile.at[:, theirs], own_a, step, landed, near_other[way])
            if n > 0:
                forward("b", step, 0, 0, n - 1, n - 1)
        send(tile.at[:, theirs], own_a, step, swap_sem.at[step], near["c"])
        now = tile[...]
        abuf[step, akey(0, 0), mine, :] = tile[:, mine]
        sums[0, 2 * step: 2 * step + 1] = fold(now * now)
        sums[0, 2 * step + 1: 2 * step + 2] = fold(now * diag)
        if step == 1:
            tr_start(0)
        for n, (kind, i, j, p) in enumerate(ORDER):
            arrive(place(kind, step, i, j, p), sem_of(kind, step, i, j, p), step)
            forward(kind, step, i, j, p, p)
            if step == 1 and n in STAGE_AT:
                tr_finish(STAGE_AT[n])
                tr_start(STAGE_AT[n] + 1)
        arrive(abuf.at[step, akey(0, 0), theirs, :], swap_sem.at[step], step)
        acc = jnp.zeros((2 * B, 2 * B), F32)
        for k in range(NK // 2):
            a = jnp.concatenate([abuf[step, 2 * k], abuf[step, 2 * k + 1]], axis=1)
            b = jnp.concatenate([bbuf[step, 2 * k], bbuf[step, 2 * k + 1]], axis=0)
            ah, al = split(a)
            bh, bl = split(b)
            acc += (jnp.dot(ah, bh, preferred_element_type=F32) + jnp.dot(al, bh, preferred_element_type=F32)
                    + jnp.dot(ah, bl, preferred_element_type=F32))
        part[step] = acc
        send(part.at[step, theirs, :], gift.at[step], step, gift_sem.at[step], near["c"])
        arrive(gift.at[step], gift_sem.at[step], step)
        if step == 1:
            tr_finish(3)
        product = part[step, mine, :] + gift[step]
        w = choice_ref[step].astype(F32)
        for h in range(2):
            lanes = slice(h * B, (h + 1) * B)
            new = mask[h] * ((1.0 - 2.0 * w) * product[:, lanes] + 2.0 * w * now[:, lanes])
            if step == STEPS - 1:
                out_ref[:, lanes] = new
            else:
                bbuf[step + 1, bkey(0, 0), :, lanes] = new
        for copy in pending:
            copy.wait_send()
        pending.clear()
    for _, copy in tr_copies:
        copy.wait_send()
    for step in range(STEPS):
        w = choice_ref[step].astype(F32)
        square, plain = jnp.sum(sums[4, 2 * step: 2 * step + 1]), jnp.sum(sums[4, 2 * step + 1: 2 * step + 2])
        tr_ref[step] = (1.0 - 2.0 * w) * square + 2.0 * w * plain


def shards(density, pattern, step_choices):
    vmem, smem = (pl.BlockSpec(memory_space=m) for m in (pltpu.VMEM, pltpu.SMEM))
    dma = pltpu.SemaphoreType.DMA
    return pl.pallas_call(
        kernel,
        out_shape=(jax.ShapeDtypeStruct(density.shape, F32), jax.ShapeDtypeStruct((STEPS,), F32)),
        in_specs=[smem, smem, pl.BlockSpec(memory_space=pl.ANY)],
        out_specs=(vmem, smem),
        scratch_shapes=[
            pltpu.VMEM((STEPS, NK, 2 * B, B), F32),
            pltpu.VMEM((STEPS, NK, B, 2 * B), F32),
            pltpu.VMEM((STEPS, 2 * B, 2 * B), F32),
            pltpu.VMEM((STEPS, B, 2 * B), F32),
            pltpu.VMEM((5, 8, 128), F32),
            pltpu.VMEM((4, 7, 8, 128), F32),
            dma((STEPS, NZ, NL, NP)),
            dma((STEPS, NH, NX, NP)),
            dma((STEPS,)),
            dma((STEPS,)),
            dma((4, 7)),
            dma((STEPS, NSEND)),
            dma((4, 7)),
            dma(()),
        ],
        compiler_params=pltpu.CompilerParams(collective_id=0, has_side_effects=True),
    )(step_choices, pattern, density)


def solution(mesh):
    return jax.shard_map(
        shards,
        mesh=mesh,
        in_specs=(P("row", "col"), P("row", "col"), P()),
        out_specs=(P("row", "col"), P()),
        check_vma=False,
    )
```

```python
import jax
import jax.numpy as jnp
from jax import lax
from jax.experimental import pallas as pl
from jax.experimental.pallas import tpu as pltpu
from jax.sharding import PartitionSpec as P

B = 128
STEPS = 2
NZ, NL, NH, NX = 8, 2, 4, 4
NK = NZ * NL
NP = 2
CROSS = (0, 3, 5)
MESH = pl.DeviceIdType.MESH
F32 = jnp.float32


def row_route(d, s, p):
    low = p < NP // 2
    go = []
    if s == 0:
        if d == 0:
            go += ["zp", "zm"]
        elif d in (1, 2) or (d == 3 and low):
            go += ["zp"]
        elif d in (7, 6) or (d == 5 and not low):
            go += ["zm"]
        if d in CROSS:
            go += ["yc"]
    else:
        if d == 0:
            go += ["zp", "zm"]
        else:
            nxt, prv = (d + 1) % NZ, (d - 1) % NZ
            if d < 4 and nxt not in CROSS and (d < 3 or low):
                go += ["zp"]
            if d > 4 and prv not in CROSS and (d > 5 or not low):
                go += ["zm"]
    return go


def col_route(e, g, p):
    low = p < NP // 2
    go = []
    if g == 0:
        if e == 0:
            go += ["yp", "ym"]
        elif e == 1 and low:
            go += ["yp"]
        elif e == 3 and not low:
            go += ["ym"]
        go += ["xp", "xm"]
    elif g == 1 and low:
        go += ["xp"]
    elif g == 3 and not low:
        go += ["xm"]
    return go


def landing(kind, i, j, way):
    if kind == "a":
        if way == "yc":
            return i, 1 - j
        return ((i + (1 if way == "zp" else -1)) % NZ, j)
    if way[0] == "y":
        return ((i + (1 if way == "yp" else -1)) % NH, j)
    return (i, (j + (1 if way == "xp" else -1)) % NX)


ORDER = [
    ("b", 0, 3, 0), ("a", 7, 0, 0), ("a", 1, 0, 0), ("b", 0, 1, 0), ("a", 7, 0, 1), ("b", 1, 0, 0),
    ("a", 1, 0, 1), ("b", 3, 0, 0), ("a", 2, 0, 0), ("b", 3, 0, 1), ("b", 1, 0, 1), ("a", 6, 0, 0),
    ("b", 0, 1, 1), ("a", 6, 0, 1), ("a", 2, 0, 1), ("a", 0, 1, 0), ("a", 0, 1, 1), ("b", 1, 1, 0),
    ("b", 0, 3, 1), ("a", 3, 0, 0), ("b", 3, 1, 0), ("b", 1, 3, 0), ("b", 2, 0, 0), ("a", 5, 0, 1),
    ("b", 2, 0, 1), ("b", 3, 3, 1), ("a", 5, 0, 0), ("a", 3, 0, 1), ("b", 1, 3, 1), ("a", 7, 1, 0),
    ("a", 1, 1, 0), ("b", 3, 3, 0), ("a", 3, 1, 0), ("a", 7, 1, 1), ("b", 1, 2, 0), ("b", 3, 2, 0),
    ("a", 1, 1, 1), ("b", 3, 1, 1), ("a", 5, 1, 1), ("b", 2, 1, 0), ("a", 4, 0, 0), ("b", 2, 3, 0),
    ("b", 0, 2, 1), ("b", 2, 3, 1), ("a", 6, 1, 0), ("a", 2, 1, 0), ("a", 4, 0, 1), ("b", 1, 1, 1),
    ("a", 6, 1, 1), ("a", 5, 1, 0), ("a", 3, 1, 1), ("a", 4, 1, 0), ("a", 2, 1, 1), ("b", 1, 2, 1),
    ("a", 4, 1, 1), ("b", 2, 1, 1), ("b", 0, 2, 0), ("b", 2, 2, 0), ("b", 3, 2, 1), ("b", 2, 2, 1),
]
assert len(ORDER) == len(set(ORDER)) == 2 * (NK - 1) * NP
STAGE_AT = {9: 0, 29: 1, 54: 2}
NSEND = 80 * NP


def split(v):
    hi = v.astype(jnp.bfloat16)
    return hi, (v - hi.astype(F32)).astype(jnp.bfloat16)


def fold(v):
    rows = jnp.sum(v, axis=0, keepdims=True)
    return rows[:, :128] + rows[:, 128:]


def kernel(choice_ref, pat_ref, x_ref, out_ref, tr_ref, abuf, bbuf, part, gift, sums, got,
           asem, bsem, swap_sem, gift_sem, tr_sem, send_sem, tr_send, fetch_sem, half):
    row, col = lax.axis_index("row"), lax.axis_index("col")
    core, x, yh = row % 2, (row // 2) % NX, row // (2 * NX)
    yl, z = col % NL, col // NL

    def at(core_=None, x_=None, yh_=None, yl_=None, z_=None):
        c = core if core_ is None else core_
        xx = x if x_ is None else x_
        h = yh if yh_ is None else yh_
        l = yl if yl_ is None else yl_
        zz = z if z_ is None else z_
        return ((h * NX + xx) * 2 + c, zz * NL + l)

    near = {
        "zp": at(z_=(z + 1) % NZ),
        "zm": at(z_=(z + NZ - 1) % NZ),
        "yc": at(yl_=1 - yl),
        "yp": at(yh_=(yh + 1) % NH),
        "ym": at(yh_=(yh + NH - 1) % NH),
        "xp": at(x_=(x + 1) % NX),
        "xm": at(x_=(x + NX - 1) % NX),
        "c": at(core_=1 - core),
    }
    near_other = {
        "zp": at(core_=1 - core, z_=(z + 1) % NZ),
        "zm": at(core_=1 - core, z_=(z + NZ - 1) % NZ),
        "yc": at(core_=1 - core, yl_=1 - yl),
    }
    def akey(d, s):
        return ((z + NZ - d) % NZ) * NL + (yl if s == 0 else 1 - yl)

    def bkey(e, g):
        return ((yh + NH - e) % NH) * NX + (x + NX - g) % NX

    barrier = pltpu.get_barrier_semaphore()
    greeted = [*near.values(), *near_other.values()]
    for place in greeted:
        pl.semaphore_signal(barrier, inc=1, device_id=place, device_id_type=MESH)
    sums[0] = jnp.zeros((8, 128), F32)
    fetch = pltpu.make_async_copy(x_ref, bbuf.at[0, bkey(0, 0)], fetch_sem)
    fetch.start()
    pl.semaphore_wait(barrier, len(greeted))
    fetch.wait()

    AR, BR = 2 * B // NP, B // NP

    def place(kind, step, i, j, p):
        if kind == "a":
            return abuf.at[step, akey(i, j), pl.ds(p * AR, AR), :]
        return bbuf.at[step, bkey(i, j), pl.ds(p * BR, BR), :]

    def sem_of(kind, step, i, j, p):
        return asem.at[step, i, j, p] if kind == "a" else bsem.at[step, i, j, p]

    pending = []

    def send(src, dst, step, recv_sem, where):
        copy = pltpu.make_async_remote_copy(
            src_ref=src, dst_ref=dst, send_sem=send_sem.at[step, len(pending)], recv_sem=recv_sem,
            device_id=where, device_id_type=MESH)
        copy.start()
        pending.append(copy)

    def arrive(ref, sem, step):
        pltpu.make_async_remote_copy(
            src_ref=ref, dst_ref=ref, send_sem=send_sem.at[step, NSEND - 1], recv_sem=sem,
            device_id=near["c"], device_id_type=MESH).wait_recv()

    def forward(kind, step, i, j, p, p_route):
        here = place(kind, step, i, j, p)
        for way in (row_route if kind == "a" else col_route)(i, j, p_route):
            ii, jj = landing(kind, i, j, way)
            send(here, here, step, sem_of(kind, step, ii, jj, p), near[way])

    mine = pl.ds(core * B, B)
    theirs = pl.ds((1 - core) * B, B)
    off = row * B - col * 2 * B
    diag = (lax.broadcasted_iota(jnp.int32, (B, 2 * B), 0) + off
            == lax.broadcasted_iota(jnp.int32, (B, 2 * B), 1)).astype(F32)
    mask = [pat_ref[0, h].astype(F32) for h in range(2)]

    groups = [
        [at(z_=(z + i) % NZ) for i in range(1, NZ)],
        [at(x_=(x + i) % NX, yl_=(yl + j) % NL) for i in range(NX) for j in range(NL) if i or j],
        [at(yh_=(yh + i) % NH) for i in range(1, NH)],
        [near["c"]],
    ]
    tr_copies = []

    def tr_start(stage):
        for n, where in enumerate(groups[stage]):
            copy = pltpu.make_async_remote_copy(
                src_ref=sums.at[stage], dst_ref=got.at[stage, n], send_sem=tr_send.at[stage, n],
                recv_sem=tr_sem.at[stage, n], device_id=where, device_id_type=MESH)
            copy.start()
            tr_copies.append((stage, copy))

    def tr_finish(stage):
        total = sums[stage]
        for n, (_, copy) in enumerate([c for c in tr_copies if c[0] == stage]):
            copy.wait_recv()
            total = total + got[stage, n]
        sums[stage + 1] = total

    for step in range(STEPS):
        tile = bbuf.at[step, bkey(0, 0)]
        for p in range(NP):
            forward("b", step, 0, 0, p, p)
        own_a = abuf.at[step, akey(0, 0), mine, :]
        other = half.at[step]
        abuf[step, akey(0, 0), mine, :] = tile[:, mine]
        half[step] = tile[:, theirs]
        for way in row_route(0, 0, 0):
            landed = asem.at[step, *landing("a", 0, 0, way), core]
            send(own_a, own_a, step, landed, near[way])
        for way in row_route(0, 0, 0):
            landed = asem.at[step, *landing("a", 0, 0, way), core]
            send(other, own_a, step, landed, near_other[way])
        send(other, own_a, step, swap_sem.at[step], near["c"])
        now = tile[...]
        sums[0, 2 * step: 2 * step + 1] = fold(now * now)
        sums[0, 2 * step + 1: 2 * step + 2] = fold(now * diag)
        if step == 1:
            tr_start(0)
        for n, (kind, i, j, p) in enumerate(ORDER):
            arrive(place(kind, step, i, j, p), sem_of(kind, step, i, j, p), step)
            forward(kind, step, i, j, p, p)
            if step == 1 and n in STAGE_AT:
                tr_finish(STAGE_AT[n])
                tr_start(STAGE_AT[n] + 1)
        arrive(abuf.at[step, akey(0, 0), theirs, :], swap_sem.at[step], step)
        acc = jnp.zeros((2 * B, 2 * B), F32)
        for k in range(NK // 2):
            a = jnp.concatenate([abuf[step, 2 * k], abuf[step, 2 * k + 1]], axis=1)
            b = jnp.concatenate([bbuf[step, 2 * k], bbuf[step, 2 * k + 1]], axis=0)
            ah, al = split(a)
            bh, bl = split(b)
            acc += (jnp.dot(ah, bh, preferred_element_type=F32) + jnp.dot(al, bh, preferred_element_type=F32)
                    + jnp.dot(ah, bl, preferred_element_type=F32))
        part[step] = acc
        send(part.at[step, theirs, :], gift.at[step], step, gift_sem.at[step], near["c"])
        arrive(gift.at[step], gift_sem.at[step], step)
        if step == 1:
            tr_finish(3)
        product = part[step, mine, :] + gift[step]
        w = choice_ref[step].astype(F32)
        for h in range(2):
            lanes = slice(h * B, (h + 1) * B)
            new = mask[h] * ((1.0 - 2.0 * w) * product[:, lanes] + 2.0 * w * now[:, lanes])
            if step == STEPS - 1:
                out_ref[:, lanes] = new
            else:
                bbuf[step + 1, bkey(0, 0), :, lanes] = new
        for copy in pending:
            copy.wait_send()
        pending.clear()
    for _, copy in tr_copies:
        copy.wait_send()
    for step in range(STEPS):
        w = choice_ref[step].astype(F32)
        square, plain = jnp.sum(sums[4, 2 * step: 2 * step + 1]), jnp.sum(sums[4, 2 * step + 1: 2 * step + 2])
        tr_ref[step] = (1.0 - 2.0 * w) * square + 2.0 * w * plain


def shards(density, pattern, step_choices):
    vmem, smem = (pl.BlockSpec(memory_space=m) for m in (pltpu.VMEM, pltpu.SMEM))
    dma = pltpu.SemaphoreType.DMA
    return pl.pallas_call(
        kernel,
        out_shape=(jax.ShapeDtypeStruct(density.shape, F32), jax.ShapeDtypeStruct((STEPS,), F32)),
        in_specs=[smem, smem, pl.BlockSpec(memory_space=pl.ANY)],
        out_specs=(vmem, smem),
        scratch_shapes=[
            pltpu.VMEM((STEPS, NK, 2 * B, B), F32),
            pltpu.VMEM((STEPS, NK, B, 2 * B), F32),
            pltpu.VMEM((STEPS, 2 * B, 2 * B), F32),
            pltpu.VMEM((STEPS, B, 2 * B), F32),
            pltpu.VMEM((5, 8, 128), F32),
            pltpu.VMEM((4, 7, 8, 128), F32),
            dma((STEPS, NZ, NL, NP)),
            dma((STEPS, NH, NX, NP)),
            dma((STEPS,)),
            dma((STEPS,)),
            dma((4, 7)),
            dma((STEPS, NSEND)),
            dma((4, 7)),
            dma(()),
            pltpu.VMEM((STEPS, B, B), F32),
        ],
        compiler_params=pltpu.CompilerParams(collective_id=0, has_side_effects=True),
    )(step_choices, pattern, density)


def solution(mesh):
    return jax.shard_map(
        shards,
        mesh=mesh,
        in_specs=(P("row", "col"), P("row", "col"), P()),
        out_specs=(P("row", "col"), P()),
        check_vma=False,
    )
```

```python
import jax
import jax.numpy as jnp
from jax import lax
from jax.experimental import pallas as pl
from jax.experimental.pallas import tpu as pltpu
from jax.sharding import PartitionSpec as P

B = 128
STEPS = 2
NZ, NL, NH, NX = 8, 2, 4, 4
NK = NZ * NL
NP = 2
CROSS = (0, 3, 5)
MESH = pl.DeviceIdType.MESH
F32 = jnp.float32


def row_route(d, s, p):
    low = p < NP // 2
    go = []
    if s == 0:
        if d == 0:
            go += ["zp", "zm"]
        elif d in (1, 2) or (d == 3 and low):
            go += ["zp"]
        elif d in (7, 6) or (d == 5 and not low):
            go += ["zm"]
        if d in CROSS:
            go += ["yc"]
    else:
        if d == 0:
            go += ["zp", "zm"]
        else:
            nxt, prv = (d + 1) % NZ, (d - 1) % NZ
            if d < 4 and nxt not in CROSS and (d < 3 or low):
                go += ["zp"]
            if d > 4 and prv not in CROSS and (d > 5 or not low):
                go += ["zm"]
    return go


def col_route(e, g, p):
    low = p < NP // 2
    go = []
    if g == 0:
        if e == 0:
            go += ["yp", "ym"]
        elif e == 1 and low:
            go += ["yp"]
        elif e == 3 and not low:
            go += ["ym"]
        go += ["xp", "xm"]
    elif g == 1 and low:
        go += ["xp"]
    elif g == 3 and not low:
        go += ["xm"]
    return go


def landing(kind, i, j, way):
    if kind == "a":
        if way == "yc":
            return i, 1 - j
        return ((i + (1 if way == "zp" else -1)) % NZ, j)
    if way[0] == "y":
        return ((i + (1 if way == "yp" else -1)) % NH, j)
    return (i, (j + (1 if way == "xp" else -1)) % NX)


ORDER = [
    ("b", 0, 3, 0), ("a", 7, 0, 0), ("a", 1, 0, 0), ("b", 0, 1, 0), ("a", 7, 0, 1), ("b", 1, 0, 0),
    ("a", 1, 0, 1), ("b", 3, 0, 0), ("a", 2, 0, 0), ("b", 3, 0, 1), ("b", 1, 0, 1), ("a", 6, 0, 0),
    ("b", 0, 1, 1), ("a", 6, 0, 1), ("a", 2, 0, 1), ("a", 0, 1, 0), ("a", 0, 1, 1), ("b", 1, 1, 0),
    ("b", 0, 3, 1), ("a", 3, 0, 0), ("b", 3, 1, 0), ("b", 1, 3, 0), ("b", 2, 0, 0), ("a", 5, 0, 1),
    ("b", 2, 0, 1), ("b", 3, 3, 1), ("a", 5, 0, 0), ("a", 3, 0, 1), ("b", 1, 3, 1), ("a", 7, 1, 0),
    ("a", 1, 1, 0), ("b", 3, 3, 0), ("a", 3, 1, 0), ("a", 7, 1, 1), ("b", 1, 2, 0), ("b", 3, 2, 0),
    ("a", 1, 1, 1), ("b", 3, 1, 1), ("a", 5, 1, 1), ("b", 2, 1, 0), ("a", 4, 0, 0), ("b", 2, 3, 0),
    ("b", 0, 2, 1), ("b", 2, 3, 1), ("a", 6, 1, 0), ("a", 2, 1, 0), ("a", 4, 0, 1), ("b", 1, 1, 1),
    ("a", 6, 1, 1), ("a", 5, 1, 0), ("a", 3, 1, 1), ("a", 4, 1, 0), ("a", 2, 1, 1), ("b", 1, 2, 1),
    ("a", 4, 1, 1), ("b", 2, 1, 1), ("b", 0, 2, 0), ("b", 2, 2, 0), ("b", 3, 2, 1), ("b", 2, 2, 1),
]
assert len(ORDER) == len(set(ORDER)) == 2 * (NK - 1) * NP
STAGE_AT = {9: 0, 29: 1, 54: 2}
GAPS = {3: 4, 4: 1, 7: 3, 8: 1, 12: 4, 13: 1, 15: 2, 18: 3, 21: 3, 23: 2, 28: 5, 31: 3, 32: 1, 37: 5, 42: 5, 47: 5, 51: 4, 58: 7}
NSEND = 80 * NP


def split(v):
    hi = v.astype(jnp.bfloat16)
    return hi, (v - hi.astype(F32)).astype(jnp.bfloat16)


def fold(v):
    rows = jnp.sum(v, axis=0, keepdims=True)
    return rows[:, :128] + rows[:, 128:]


def kernel(choice_hbm, pat_hbm, x_ref, out_ref, tr_ref, abuf, bbuf, part, gift, sums, got,
           asem, bsem, swap_sem, gift_sem, tr_sem, send_sem, tr_send, fetch_sem, half, choice_ref, pat_ref, ahi, alo, bhi, blo):
    row, col = lax.axis_index("row"), lax.axis_index("col")
    core, x, yh = row % 2, (row // 2) % NX, row // (2 * NX)
    yl, z = col % NL, col // NL

    def at(core_=None, x_=None, yh_=None, yl_=None, z_=None):
        c = core if core_ is None else core_
        xx = x if x_ is None else x_
        h = yh if yh_ is None else yh_
        l = yl if yl_ is None else yl_
        zz = z if z_ is None else z_
        return ((h * NX + xx) * 2 + c, zz * NL + l)

    near = {
        "zp": at(z_=(z + 1) % NZ),
        "zm": at(z_=(z + NZ - 1) % NZ),
        "yc": at(yl_=1 - yl),
        "yp": at(yh_=(yh + 1) % NH),
        "ym": at(yh_=(yh + NH - 1) % NH),
        "xp": at(x_=(x + 1) % NX),
        "xm": at(x_=(x + NX - 1) % NX),
        "c": at(core_=1 - core),
    }
    near_other = {
        "zp": at(core_=1 - core, z_=(z + 1) % NZ),
        "zm": at(core_=1 - core, z_=(z + NZ - 1) % NZ),
        "yc": at(core_=1 - core, yl_=1 - yl),
    }
    def akey(d, s):
        return ((z + NZ - d) % NZ) * NL + (yl if s == 0 else 1 - yl)

    def bkey(e, g):
        return ((yh + NH - e) % NH) * NX + (x + NX - g) % NX

    barrier = pltpu.get_barrier_semaphore()
    greeted = [*near.values(), *near_other.values()]
    for place in greeted:
        pl.semaphore_signal(barrier, inc=1, device_id=place, device_id_type=MESH)
    sums[0] = jnp.zeros((8, 128), F32)
    fetch = pltpu.make_async_copy(x_ref, bbuf.at[0, bkey(0, 0)], fetch_sem.at[0])
    fetch.start()
    small = [
        pltpu.make_async_copy(choice_hbm, choice_ref, fetch_sem.at[1]),
        pltpu.make_async_copy(pat_hbm, pat_ref, fetch_sem.at[2]),
    ]
    for copy in small:
        copy.start()
    pl.semaphore_wait(barrier, len(greeted))
    fetch.wait()

    AR, BR = 2 * B // NP, B // NP

    def place(kind, step, i, j, p):
        if kind == "a":
            return abuf.at[step, akey(i, j), pl.ds(p * AR, AR), :]
        return bbuf.at[step, bkey(i, j), pl.ds(p * BR, BR), :]

    def sem_of(kind, step, i, j, p):
        return asem.at[step, i, j, p] if kind == "a" else bsem.at[step, i, j, p]

    pending = []

    def send(src, dst, step, recv_sem, where):
        copy = pltpu.make_async_remote_copy(
            src_ref=src, dst_ref=dst, send_sem=send_sem.at[step, len(pending)], recv_sem=recv_sem,
            device_id=where, device_id_type=MESH)
        copy.start()
        pending.append(copy)

    def arrive(ref, sem, step):
        pltpu.make_async_remote_copy(
            src_ref=ref, dst_ref=ref, send_sem=send_sem.at[step, NSEND - 1], recv_sem=sem,
            device_id=near["c"], device_id_type=MESH).wait_recv()

    def forward(kind, step, i, j, p, p_route):
        here = place(kind, step, i, j, p)
        for way in (row_route if kind == "a" else col_route)(i, j, p_route):
            ii, jj = landing(kind, i, j, way)
            send(here, here, step, sem_of(kind, step, ii, jj, p), near[way])

    def halve(kind, step, i, j, rows):
        key = akey(i, j) if kind == "a" else bkey(i, j)
        whole, hi, lo = (abuf, ahi, alo) if kind == "a" else (bbuf, bhi, blo)
        hi[key, rows, :], lo[key, rows, :] = split(whole[step, key, rows, :])

    mine = pl.ds(core * B, B)
    theirs = pl.ds((1 - core) * B, B)
    off = row * B - col * 2 * B
    diag = (lax.broadcasted_iota(jnp.int32, (B, 2 * B), 0) + off
            == lax.broadcasted_iota(jnp.int32, (B, 2 * B), 1)).astype(F32)

    groups = [
        [at(z_=(z + i) % NZ) for i in range(1, NZ)],
        [at(x_=(x + i) % NX, yl_=(yl + j) % NL) for i in range(NX) for j in range(NL) if i or j],
        [at(yh_=(yh + i) % NH) for i in range(1, NH)],
        [near["c"]],
    ]

    def tr_copies(stage):
        return [
            pltpu.make_async_remote_copy(
                src_ref=sums.at[stage], dst_ref=got.at[stage, n], send_sem=tr_send.at[stage, n],
                recv_sem=tr_sem.at[stage, n], device_id=where, device_id_type=MESH)
            for n, where in enumerate(groups[stage])
        ]

    def tr_start(stage):
        for copy in tr_copies(stage):
            copy.start()

    def tr_finish(stage):
        total = sums[stage]
        for n, copy in enumerate(tr_copies(stage)):
            copy.wait_recv()
            total = total + got[stage, n]
        sums[stage + 1] = total

    def advance(step, _):
        tile = bbuf.at[step, bkey(0, 0)]
        for p in range(NP):
            forward("b", step, 0, 0, p, p)
        own_a = abuf.at[step, akey(0, 0), mine, :]
        other = half.at[step]
        abuf[step, akey(0, 0), mine, :] = tile[:, mine]
        half[step] = tile[:, theirs]
        for way in row_route(0, 0, 0):
            landed = asem.at[step, *landing("a", 0, 0, way), core]
            send(own_a, own_a, step, landed, near[way])
        for way in row_route(0, 0, 0):
            landed = asem.at[step, *landing("a", 0, 0, way), core]
            send(other, own_a, step, landed, near_other[way])
        send(other, own_a, step, swap_sem.at[step], near["c"])
        now = tile[...]
        halve("b", step, 0, 0, pl.ds(0, B))
        halve("a", step, 0, 0, mine)
        sums[0, pl.ds(2 * step, 1)] = fold(now * now)
        sums[0, pl.ds(2 * step + 1, 1)] = fold(now * diag)

        @pl.when(step == STEPS - 1)
        def _():
            tr_start(0)

        waiting = []
        for n, (kind, i, j, p) in enumerate(ORDER):
            arrive(place(kind, step, i, j, p), sem_of(kind, step, i, j, p), step)
            forward(kind, step, i, j, p, p)
            waiting.append((kind, i, j, p))
            for _ in range(len(waiting) if n + 1 == len(ORDER) else min(len(waiting), GAPS.get(n, 0))):
                kind, i, j, p = waiting.pop(0)
                halve(kind, step, i, j, pl.ds(p * AR, AR) if kind == "a" else pl.ds(p * BR, BR))
            if n in STAGE_AT:
                @pl.when(step == STEPS - 1)
                def _():
                    tr_finish(STAGE_AT[n])
                    tr_start(STAGE_AT[n] + 1)
        arrive(abuf.at[step, akey(0, 0), theirs, :], swap_sem.at[step], step)
        halve("a", step, 0, 0, theirs)

        def product_of(rows):
            left_hi = jnp.concatenate([ahi[k, rows, :] for k in range(NK)], axis=1)
            left_lo = jnp.concatenate([alo[k, rows, :] for k in range(NK)], axis=1)
            right_hi = jnp.concatenate([bhi[k] for k in range(NK)], axis=0)
            right_lo = jnp.concatenate([blo[k] for k in range(NK)], axis=0)
            return (jnp.dot(left_hi, right_hi, preferred_element_type=F32)
                    + jnp.dot(left_lo, right_hi, preferred_element_type=F32)
                    + jnp.dot(left_hi, right_lo, preferred_element_type=F32))

        part[step, theirs, :] = product_of(theirs)
        send(part.at[step, theirs, :], gift.at[step], step, gift_sem.at[step], near["c"])
        part[step, mine, :] = product_of(mine)
        for copy in pending[:-1]:
            copy.wait_send()
        arrive(gift.at[step], gift_sem.at[step], step)

        @pl.when(step == STEPS - 1)
        def _():
            tr_finish(3)

        product = part[step, mine, :] + gift[step]

        @pl.when(step == 0)
        def _():
            for copy in small:
                copy.wait()

        mask = [pat_ref[0, h].astype(F32) for h in range(2)]
        w = choice_ref[step].astype(F32)
        for h in range(2):
            lanes = slice(h * B, (h + 1) * B)
            new = mask[h] * ((1.0 - 2.0 * w) * product[:, lanes] + 2.0 * w * now[:, lanes])
            bbuf[step + 1, bkey(0, 0), :, lanes] = new
        pending[-1].wait_send()
        pending.clear()
        return 0

    lax.fori_loop(0, STEPS, advance, 0)
    store = pltpu.make_async_copy(bbuf.at[STEPS, bkey(0, 0)], out_ref, fetch_sem.at[0])
    store.start()
    for stage in range(len(groups)):
        for copy in tr_copies(stage):
            copy.wait_send()
    for step in range(STEPS):
        w = choice_ref[step].astype(F32)
        square, plain = jnp.sum(sums[4, 2 * step: 2 * step + 1]), jnp.sum(sums[4, 2 * step + 1: 2 * step + 2])
        tr_ref[step] = (1.0 - 2.0 * w) * square + 2.0 * w * plain
    store.wait()


def shards(density, pattern, step_choices):
    smem = pl.BlockSpec(memory_space=pltpu.SMEM)
    dma = pltpu.SemaphoreType.DMA
    return pl.pallas_call(
        kernel,
        out_shape=(jax.ShapeDtypeStruct(density.shape, F32), jax.ShapeDtypeStruct((STEPS,), F32)),
        in_specs=[pl.BlockSpec(memory_space=pltpu.HBM)] * 3,
        out_specs=(pl.BlockSpec(memory_space=pl.ANY), smem),
        scratch_shapes=[
            pltpu.VMEM((STEPS, NK, 2 * B, B), F32),
            pltpu.VMEM((STEPS + 1, NK, B, 2 * B), F32),
            pltpu.VMEM((STEPS, 2 * B, 2 * B), F32),
            pltpu.VMEM((STEPS, B, 2 * B), F32),
            pltpu.VMEM((5, 8, 128), F32),
            pltpu.VMEM((4, 7, 8, 128), F32),
            dma((STEPS, NZ, NL, NP)),
            dma((STEPS, NH, NX, NP)),
            dma((STEPS,)),
            dma((STEPS,)),
            dma((4, 7)),
            dma((STEPS, NSEND)),
            dma((4, 7)),
            dma((3,)),
            pltpu.VMEM((STEPS, B, B), F32),
            pltpu.SMEM((STEPS,), jnp.int32),
            pltpu.SMEM((1, 2), jnp.int32),
            *[pltpu.VMEM((NK, 2 * B, B), jnp.bfloat16)] * 2,
            *[pltpu.VMEM((NK, B, 2 * B), jnp.bfloat16)] * 2,
        ],
        compiler_params=pltpu.CompilerParams(collective_id=0, has_side_effects=True),
    )(step_choices, pattern, density)


def solution(mesh):
    return jax.shard_map(
        shards,
        mesh=mesh,
        in_specs=(P("row", "col"), P("row", "col"), P()),
        out_specs=(P("row", "col"), P()),
        check_vma=False,
    )
```

```python
import jax
import jax.numpy as jnp
from jax import lax
from jax.experimental import pallas as pl
from jax.experimental.pallas import tpu as pltpu
from jax.sharding import PartitionSpec as P

B = 128
STEPS = 2
NZ, NL, NH, NX = 8, 2, 4, 4
NK = NZ * NL
NP = 2
CROSS = (0, 3, 5)
MESH = pl.DeviceIdType.MESH
F32 = jnp.float32


def row_route(d, s, p):
    low = p < NP // 2
    go = []
    if s == 0:
        if d == 0:
            go += ["zp", "zm"]
        elif d in (1, 2) or (d == 3 and low):
            go += ["zp"]
        elif d in (7, 6) or (d == 5 and not low):
            go += ["zm"]
        if d in CROSS:
            go += ["yc"]
    else:
        if d == 0:
            go += ["zp", "zm"]
        else:
            nxt, prv = (d + 1) % NZ, (d - 1) % NZ
            if d < 4 and nxt not in CROSS and (d < 3 or low):
                go += ["zp"]
            if d > 4 and prv not in CROSS and (d > 5 or not low):
                go += ["zm"]
    return go


def col_route(e, g, p):
    low = p < NP // 2
    go = []
    if g == 0:
        if e == 0:
            go += ["yp", "ym"]
        elif e == 1 and low:
            go += ["yp"]
        elif e == 3 and not low:
            go += ["ym"]
        go += ["xp", "xm"]
    elif g == 1 and low:
        go += ["xp"]
    elif g == 3 and not low:
        go += ["xm"]
    return go


def landing(kind, i, j, way):
    if kind == "a":
        if way == "yc":
            return i, 1 - j
        return ((i + (1 if way == "zp" else -1)) % NZ, j)
    if way[0] == "y":
        return ((i + (1 if way == "yp" else -1)) % NH, j)
    return (i, (j + (1 if way == "xp" else -1)) % NX)


ORDER = [
    ("b", 0, 3, 0), ("a", 7, 0, 0), ("a", 1, 0, 0), ("b", 0, 1, 0), ("a", 7, 0, 1), ("b", 1, 0, 0),
    ("a", 1, 0, 1), ("b", 3, 0, 0), ("a", 2, 0, 0), ("b", 3, 0, 1), ("b", 1, 0, 1), ("a", 6, 0, 0),
    ("b", 0, 1, 1), ("a", 6, 0, 1), ("a", 2, 0, 1), ("a", 0, 1, 0), ("a", 0, 1, 1), ("b", 1, 1, 0),
    ("b", 0, 3, 1), ("a", 3, 0, 0), ("b", 3, 1, 0), ("b", 1, 3, 0), ("b", 2, 0, 0), ("a", 5, 0, 1),
    ("b", 2, 0, 1), ("b", 3, 3, 1), ("a", 5, 0, 0), ("a", 3, 0, 1), ("b", 1, 3, 1), ("a", 7, 1, 0),
    ("a", 1, 1, 0), ("b", 3, 3, 0), ("a", 3, 1, 0), ("a", 7, 1, 1), ("b", 1, 2, 0), ("b", 3, 2, 0),
    ("a", 1, 1, 1), ("b", 3, 1, 1), ("a", 5, 1, 1), ("b", 2, 1, 0), ("a", 4, 0, 0), ("b", 2, 3, 0),
    ("b", 0, 2, 1), ("b", 2, 3, 1), ("a", 6, 1, 0), ("a", 2, 1, 0), ("a", 4, 0, 1), ("b", 1, 1, 1),
    ("a", 6, 1, 1), ("a", 5, 1, 0), ("a", 3, 1, 1), ("a", 4, 1, 0), ("a", 2, 1, 1), ("b", 1, 2, 1),
    ("a", 4, 1, 1), ("b", 2, 1, 1), ("b", 0, 2, 0), ("b", 2, 2, 0), ("b", 3, 2, 1), ("b", 2, 2, 1),
]
assert len(ORDER) == len(set(ORDER)) == 2 * (NK - 1) * NP
STAGE_AT = {9: 0, 29: 1, 54: 2}
GAPS = {3: 4, 4: 1, 7: 3, 8: 1, 12: 4, 13: 1, 15: 2, 18: 3, 21: 3, 23: 2, 28: 5, 31: 3, 32: 1, 37: 5, 42: 5, 47: 5, 51: 4, 58: 7}
NSEND = 80 * NP


def split(v):
    hi = v.astype(jnp.bfloat16)
    return hi, (v - hi.astype(F32)).astype(jnp.bfloat16)


def fold(v):
    rows = jnp.sum(v, axis=0, keepdims=True)
    return rows[:, :128] + rows[:, 128:]


def kernel(choice_hbm, pat_hbm, x_ref, out_ref, tr_ref, abuf, bbuf, part, gift, sums, got,
           asem, bsem, swap_sem, gift_sem, tr_sem, send_sem, tr_send, fetch_sem, half, choice_ref, pat_ref, ahi, alo, bhi, blo):
    row, col = lax.axis_index("row"), lax.axis_index("col")
    core, x, yh = row % 2, (row // 2) % NX, row // (2 * NX)
    yl, z = col % NL, col // NL

    def at(core_=None, x_=None, yh_=None, yl_=None, z_=None):
        c = core if core_ is None else core_
        xx = x if x_ is None else x_
        h = yh if yh_ is None else yh_
        l = yl if yl_ is None else yl_
        zz = z if z_ is None else z_
        return ((h * NX + xx) * 2 + c, zz * NL + l)

    near = {
        "zp": at(z_=(z + 1) % NZ),
        "zm": at(z_=(z + NZ - 1) % NZ),
        "yc": at(yl_=1 - yl),
        "yp": at(yh_=(yh + 1) % NH),
        "ym": at(yh_=(yh + NH - 1) % NH),
        "xp": at(x_=(x + 1) % NX),
        "xm": at(x_=(x + NX - 1) % NX),
        "c": at(core_=1 - core),
    }
    near_other = {
        "zp": at(core_=1 - core, z_=(z + 1) % NZ),
        "zm": at(core_=1 - core, z_=(z + NZ - 1) % NZ),
        "yc": at(core_=1 - core, yl_=1 - yl),
    }
    def akey(d, s):
        return ((z + NZ - d) % NZ) * NL + (yl if s == 0 else 1 - yl)

    def bkey(e, g):
        return ((yh + NH - e) % NH) * NX + (x + NX - g) % NX

    barrier = pltpu.get_barrier_semaphore()
    greeted = [*near.values(), *near_other.values()]
    for place in greeted:
        pl.semaphore_signal(barrier, inc=1, device_id=place, device_id_type=MESH)
    sums[0] = jnp.zeros((8, 128), F32)
    fetch = pltpu.make_async_copy(x_ref, bbuf.at[0, bkey(0, 0)], fetch_sem.at[0])
    fetch.start()
    small = [
        pltpu.make_async_copy(choice_hbm, choice_ref, fetch_sem.at[1]),
        pltpu.make_async_copy(pat_hbm, pat_ref, fetch_sem.at[2]),
    ]
    for copy in small:
        copy.start()
    pl.semaphore_wait(barrier, len(greeted))
    fetch.wait()

    AR, BR = 2 * B // NP, B // NP

    def place(kind, step, i, j, p):
        if kind == "a":
            return abuf.at[step, akey(i, j), pl.ds(p * AR, AR), :]
        return bbuf.at[step, bkey(i, j), pl.ds(p * BR, BR), :]

    def sem_of(kind, step, i, j, p):
        return asem.at[step, i, j, p] if kind == "a" else bsem.at[step, i, j, p]

    pending = []

    def send(src, dst, step, recv_sem, where):
        copy = pltpu.make_async_remote_copy(
            src_ref=src, dst_ref=dst, send_sem=send_sem.at[step, len(pending)], recv_sem=recv_sem,
            device_id=where, device_id_type=MESH)
        copy.start()
        pending.append(copy)

    def arrive(ref, sem, step):
        pltpu.make_async_remote_copy(
            src_ref=ref, dst_ref=ref, send_sem=send_sem.at[step, NSEND - 1], recv_sem=sem,
            device_id=near["c"], device_id_type=MESH).wait_recv()

    def forward(kind, step, i, j, p, p_route):
        here = place(kind, step, i, j, p)
        for way in (row_route if kind == "a" else col_route)(i, j, p_route):
            ii, jj = landing(kind, i, j, way)
            send(here, here, step, sem_of(kind, step, ii, jj, p), near[way])

    def halve(kind, step, i, j, rows):
        key = akey(i, j) if kind == "a" else bkey(i, j)
        whole, hi, lo = (abuf, ahi, alo) if kind == "a" else (bbuf, bhi, blo)
        hi[key, rows, :], lo[key, rows, :] = split(whole[step, key, rows, :])

    mine = pl.ds(core * B, B)
    theirs = pl.ds((1 - core) * B, B)
    off = row * B - col * 2 * B
    diag = (lax.broadcasted_iota(jnp.int32, (B, 2 * B), 0) + off
            == lax.broadcasted_iota(jnp.int32, (B, 2 * B), 1)).astype(F32)

    groups = [
        [at(z_=(z + i) % NZ) for i in range(1, NZ)],
        [at(x_=(x + i) % NX, yl_=(yl + j) % NL) for i in range(NX) for j in range(NL) if i or j],
        [at(yh_=(yh + i) % NH) for i in range(1, NH)],
        [near["c"]],
    ]

    def tr_copies(stage):
        return [
            pltpu.make_async_remote_copy(
                src_ref=sums.at[stage], dst_ref=got.at[stage, n], send_sem=tr_send.at[stage, n],
                recv_sem=tr_sem.at[stage, n], device_id=where, device_id_type=MESH)
            for n, where in enumerate(groups[stage])
        ]

    def tr_start(stage):
        for copy in tr_copies(stage):
            copy.start()

    def tr_finish(stage):
        total = sums[stage]
        for n, copy in enumerate(tr_copies(stage)):
            copy.wait_recv()
            total = total + got[stage, n]
        sums[stage + 1] = total

    def advance(step, _):
        tile = bbuf.at[step, bkey(0, 0)]
        for p in range(NP):
            forward("b", step, 0, 0, p, p)
        own_a = abuf.at[step, akey(0, 0), mine, :]
        other = half.at[step]
        abuf[step, akey(0, 0), mine, :] = tile[:, mine]
        half[step] = tile[:, theirs]
        for way in row_route(0, 0, 0):
            landed = asem.at[step, *landing("a", 0, 0, way), core]
            send(own_a, own_a, step, landed, near[way])
        for way in row_route(0, 0, 0):
            landed = asem.at[step, *landing("a", 0, 0, way), core]
            send(other, own_a, step, landed, near_other[way])
        send(other, own_a, step, swap_sem.at[step], near["c"])
        now = tile[...]
        halve("b", step, 0, 0, pl.ds(0, B))
        halve("a", step, 0, 0, mine)
        sums[0, pl.ds(2 * step, 1)] = fold(now * now)
        sums[0, pl.ds(2 * step + 1, 1)] = fold(now * diag)

        @pl.when(step == STEPS - 1)
        def _():
            tr_start(0)

        waiting = []
        for n, (kind, i, j, p) in enumerate(ORDER):
            arrive(place(kind, step, i, j, p), sem_of(kind, step, i, j, p), step)
            forward(kind, step, i, j, p, p)
            waiting.append((kind, i, j, p))
            for _ in range(len(waiting) if n + 1 == len(ORDER) else min(len(waiting), GAPS.get(n, 0))):
                kind, i, j, p = waiting.pop(0)
                halve(kind, step, i, j, pl.ds(p * AR, AR) if kind == "a" else pl.ds(p * BR, BR))
            if n in STAGE_AT:
                @pl.when(step == STEPS - 1)
                def _():
                    tr_finish(STAGE_AT[n])
                    tr_start(STAGE_AT[n] + 1)
        arrive(abuf.at[step, akey(0, 0), theirs, :], swap_sem.at[step], step)
        halve("a", step, 0, 0, theirs)

        def product_of(rows):
            left_hi = jnp.concatenate([ahi[k, rows, :] for k in range(NK)], axis=1)
            left_lo = jnp.concatenate([alo[k, rows, :] for k in range(NK)], axis=1)
            right_hi = jnp.concatenate([bhi[k] for k in range(NK)], axis=0)
            right_lo = jnp.concatenate([blo[k] for k in range(NK)], axis=0)
            return (jnp.dot(left_hi, right_hi, preferred_element_type=F32)
                    + jnp.dot(left_lo, right_hi, preferred_element_type=F32)
                    + jnp.dot(left_hi, right_lo, preferred_element_type=F32))

        part[step, theirs, :] = product_of(theirs)
        send(part.at[step, theirs, :], gift.at[step], step, gift_sem.at[step], near["c"])
        part[step, mine, :] = product_of(mine)
        for copy in pending[:-1]:
            copy.wait_send()
        arrive(gift.at[step], gift_sem.at[step], step)

        @pl.when(step == STEPS - 1)
        def _():
            tr_finish(3)

        product = part[step, mine, :] + gift[step]

        @pl.when(step == 0)
        def _():
            for copy in small:
                copy.wait()

        mask = [pat_ref[0, h].astype(F32) for h in range(2)]
        w = choice_ref[step].astype(F32)
        for h in range(2):
            lanes = slice(h * B, (h + 1) * B)
            new = mask[h] * ((1.0 - 2.0 * w) * product[:, lanes] + 2.0 * w * now[:, lanes])
            bbuf[step + 1, bkey(0, 0), :, lanes] = new
        pending[-1].wait_send()
        pending.clear()
        return 0

    lax.fori_loop(0, STEPS, advance, 0)
    store = pltpu.make_async_copy(bbuf.at[STEPS, bkey(0, 0)], out_ref, fetch_sem.at[0])
    store.start()
    for stage in range(len(groups)):
        for copy in tr_copies(stage):
            copy.wait_send()
    for step in range(STEPS):
        w = choice_ref[step].astype(F32)
        square, plain = jnp.sum(sums[4, 2 * step: 2 * step + 1]), jnp.sum(sums[4, 2 * step + 1: 2 * step + 2])
        tr_ref[step] = (1.0 - 2.0 * w) * square + 2.0 * w * plain
    store.wait()


def shards(density, pattern, step_choices):
    smem = pl.BlockSpec(memory_space=pltpu.SMEM)
    dma = pltpu.SemaphoreType.DMA
    return pl.pallas_call(
        kernel,
        out_shape=(jax.ShapeDtypeStruct(density.shape, F32), jax.ShapeDtypeStruct((STEPS,), F32)),
        in_specs=[pl.BlockSpec(memory_space=pltpu.HBM)] * 3,
        out_specs=(pl.BlockSpec(memory_space=pl.ANY), smem),
        scratch_shapes=[
            pltpu.VMEM((STEPS, NK, 2 * B, B), F32),
            pltpu.VMEM((STEPS + 1, NK, B, 2 * B), F32),
            pltpu.VMEM((STEPS, 2 * B, 2 * B), F32),
            pltpu.VMEM((STEPS, B, 2 * B), F32),
            pltpu.VMEM((5, 8, 128), F32),
            pltpu.VMEM((4, 7, 8, 128), F32),
            dma((STEPS, NZ, NL, NP)),
            dma((STEPS, NH, NX, NP)),
            dma((STEPS,)),
            dma((STEPS,)),
            dma((4, 7)),
            dma((STEPS, NSEND)),
            dma((4, 7)),
            dma((3,)),
            pltpu.VMEM((STEPS, B, B), F32),
            pltpu.SMEM((STEPS,), jnp.int32),
            pltpu.SMEM((1, 2), jnp.int32),
            *[pltpu.VMEM((NK, 2 * B, B), jnp.bfloat16)] * 2,
            *[pltpu.VMEM((NK, B, 2 * B), jnp.bfloat16)] * 2,
        ],
        compiler_params=pltpu.CompilerParams(collective_id=0, has_side_effects=True, vmem_limit_bytes=24 << 20),
    )(*(pltpu.with_memory_space_constraint(v, pltpu.HBM) for v in (step_choices, pattern, density)))


def solution(mesh):
    return jax.shard_map(
        shards,
        mesh=mesh,
        in_specs=(P("row", "col"), P("row", "col"), P()),
        out_specs=(P("row", "col"), P()),
        check_vma=False,
    )
```

```python
import jax
import jax.numpy as jnp
from jax import lax
from jax.experimental import pallas as pl
from jax.experimental.pallas import tpu as pltpu
from jax.sharding import PartitionSpec as P

B = 128
STEPS = 2
NZ, NL, NH, NX = 8, 2, 4, 4
NK = NZ * NL
NP = 2
CROSS = (0, 3, 5)
MESH = pl.DeviceIdType.MESH
F32 = jnp.float32


def row_route(d, s, p):
    low = p < NP // 2
    go = []
    if s == 0:
        if d == 0:
            go += ["zp", "zm"]
        elif d in (1, 2) or (d == 3 and low):
            go += ["zp"]
        elif d in (7, 6) or (d == 5 and not low):
            go += ["zm"]
        if d in CROSS:
            go += ["yc"]
    else:
        if d == 0:
            go += ["zp", "zm"]
        else:
            nxt, prv = (d + 1) % NZ, (d - 1) % NZ
            if d < 4 and nxt not in CROSS and (d < 3 or low):
                go += ["zp"]
            if d > 4 and prv not in CROSS and (d > 5 or not low):
                go += ["zm"]
    return go


def col_route(e, g, p):
    low = p < NP // 2
    go = []
    if g == 0:
        if e == 0:
            go += ["yp", "ym"]
        elif e == 1 and low:
            go += ["yp"]
        elif e == 3 and not low:
            go += ["ym"]
        go += ["xp", "xm"]
    elif g == 1 and low:
        go += ["xp"]
    elif g == 3 and not low:
        go += ["xm"]
    return go


def landing(kind, i, j, way):
    if kind == "a":
        if way == "yc":
            return i, 1 - j
        return ((i + (1 if way == "zp" else -1)) % NZ, j)
    if way[0] == "y":
        return ((i + (1 if way == "yp" else -1)) % NH, j)
    return (i, (j + (1 if way == "xp" else -1)) % NX)


ORDER = [
    ("b", 0, 3, 0), ("a", 7, 0, 0), ("a", 1, 0, 0), ("b", 0, 1, 0), ("a", 7, 0, 1), ("b", 1, 0, 0),
    ("a", 1, 0, 1), ("b", 3, 0, 0), ("a", 2, 0, 0), ("b", 3, 0, 1), ("b", 1, 0, 1), ("a", 6, 0, 0),
    ("b", 0, 1, 1), ("a", 6, 0, 1), ("a", 2, 0, 1), ("a", 0, 1, 0), ("a", 0, 1, 1), ("b", 1, 1, 0),
    ("b", 0, 3, 1), ("a", 3, 0, 0), ("b", 3, 1, 0), ("b", 1, 3, 0), ("b", 2, 0, 0), ("a", 5, 0, 1),
    ("b", 2, 0, 1), ("b", 3, 3, 1), ("a", 5, 0, 0), ("a", 3, 0, 1), ("b", 1, 3, 1), ("a", 7, 1, 0),
    ("a", 1, 1, 0), ("b", 3, 3, 0), ("a", 3, 1, 0), ("a", 7, 1, 1), ("b", 1, 2, 0), ("b", 3, 2, 0),
    ("a", 1, 1, 1), ("b", 3, 1, 1), ("a", 5, 1, 1), ("b", 2, 1, 0), ("a", 4, 0, 0), ("b", 2, 3, 0),
    ("b", 0, 2, 1), ("b", 2, 3, 1), ("a", 6, 1, 0), ("a", 2, 1, 0), ("a", 4, 0, 1), ("b", 1, 1, 1),
    ("a", 6, 1, 1), ("a", 5, 1, 0), ("a", 3, 1, 1), ("a", 4, 1, 0), ("a", 2, 1, 1), ("b", 1, 2, 1),
    ("a", 4, 1, 1), ("b", 2, 1, 1), ("b", 0, 2, 0), ("b", 2, 2, 0), ("b", 3, 2, 1), ("b", 2, 2, 1),
]
assert len(ORDER) == len(set(ORDER)) == 2 * (NK - 1) * NP
STAGE_AT = {9: 0, 29: 1, 54: 2}
GAPS = {3: 4, 4: 1, 7: 3, 8: 1, 12: 4, 13: 1, 15: 2, 18: 3, 21: 3, 23: 2, 28: 5, 31: 3, 32: 1, 37: 5, 42: 5, 47: 5, 51: 4, 58: 7}
NSEND = 80 * NP


def split(v):
    hi = v.astype(jnp.bfloat16)
    return hi, (v - hi.astype(F32)).astype(jnp.bfloat16)


def fold(v):
    rows = jnp.sum(v, axis=0, keepdims=True)
    return rows[:, :128] + rows[:, 128:]


def kernel(choice_hbm, pat_hbm, x_ref, out_ref, tr_ref, abuf, bbuf, part, gift, sums, got,
           asem, bsem, swap_sem, gift_sem, tr_sem, send_sem, tr_send, fetch_sem, half, choice_ref, pat_ref, ahi, alo, bhi, blo):
    row, col = lax.axis_index("row"), lax.axis_index("col")
    core, x, yh = row % 2, (row // 2) % NX, row // (2 * NX)
    yl, z = col % NL, col // NL

    def at(core_=None, x_=None, yh_=None, yl_=None, z_=None):
        c = core if core_ is None else core_
        xx = x if x_ is None else x_
        h = yh if yh_ is None else yh_
        l = yl if yl_ is None else yl_
        zz = z if z_ is None else z_
        return ((h * NX + xx) * 2 + c, zz * NL + l)

    near = {
        "zp": at(z_=(z + 1) % NZ),
        "zm": at(z_=(z + NZ - 1) % NZ),
        "yc": at(yl_=1 - yl),
        "yp": at(yh_=(yh + 1) % NH),
        "ym": at(yh_=(yh + NH - 1) % NH),
        "xp": at(x_=(x + 1) % NX),
        "xm": at(x_=(x + NX - 1) % NX),
        "c": at(core_=1 - core),
    }
    near_other = {
        "zp": at(core_=1 - core, z_=(z + 1) % NZ),
        "zm": at(core_=1 - core, z_=(z + NZ - 1) % NZ),
        "yc": at(core_=1 - core, yl_=1 - yl),
    }
    def akey(d, s):
        return ((z + NZ - d) % NZ) * NL + (yl if s == 0 else 1 - yl)

    def bkey(e, g):
        return ((yh + NH - e) % NH) * NX + (x + NX - g) % NX

    barrier = pltpu.get_barrier_semaphore()
    greeted = [*near.values(), *near_other.values()]
    for place in greeted:
        pl.semaphore_signal(barrier, inc=1, device_id=place, device_id_type=MESH)
    sums[0] = jnp.zeros((8, 128), F32)
    fetch = pltpu.make_async_copy(x_ref, bbuf.at[0, bkey(0, 0)], fetch_sem.at[0])
    fetch.start()
    small = [
        pltpu.make_async_copy(choice_hbm, choice_ref, fetch_sem.at[1]),
        pltpu.make_async_copy(pat_hbm, pat_ref, fetch_sem.at[2]),
    ]
    for copy in small:
        copy.start()
    pl.semaphore_wait(barrier, len(greeted))
    fetch.wait()

    AR, BR = 2 * B // NP, B // NP

    def place(kind, step, i, j, p):
        if kind == "a":
            return abuf.at[step, akey(i, j), pl.ds(p * AR, AR), :]
        return bbuf.at[step, bkey(i, j), pl.ds(p * BR, BR), :]

    def sem_of(kind, step, i, j, p):
        return asem.at[step, i, j, p] if kind == "a" else bsem.at[step, i, j, p]

    pending = []

    def send(src, dst, step, recv_sem, where):
        copy = pltpu.make_async_remote_copy(
            src_ref=src, dst_ref=dst, send_sem=send_sem.at[step, len(pending)], recv_sem=recv_sem,
            device_id=where, device_id_type=MESH)
        copy.start()
        pending.append(copy)

    def arrive(ref, sem, step):
        pltpu.make_async_remote_copy(
            src_ref=ref, dst_ref=ref, send_sem=send_sem.at[step, NSEND - 1], recv_sem=sem,
            device_id=near["c"], device_id_type=MESH).wait_recv()

    def forward(kind, step, i, j, p, p_route):
        here = place(kind, step, i, j, p)
        for way in (row_route if kind == "a" else col_route)(i, j, p_route):
            ii, jj = landing(kind, i, j, way)
            send(here, here, step, sem_of(kind, step, ii, jj, p), near[way])

    def halve(kind, step, i, j, rows):
        key = akey(i, j) if kind == "a" else bkey(i, j)
        whole, hi, lo = (abuf, ahi, alo) if kind == "a" else (bbuf, bhi, blo)
        hi[key, rows, :], lo[key, rows, :] = split(whole[step, key, rows, :])

    mine = pl.ds(core * B, B)
    theirs = pl.ds((1 - core) * B, B)
    off = row * B - col * 2 * B
    diag = (lax.broadcasted_iota(jnp.int32, (B, 2 * B), 0) + off
            == lax.broadcasted_iota(jnp.int32, (B, 2 * B), 1)).astype(F32)

    groups = [
        [at(z_=(z + i) % NZ) for i in range(1, NZ)],
        [at(x_=(x + i) % NX, yl_=(yl + j) % NL) for i in range(NX) for j in range(NL) if i or j],
        [at(yh_=(yh + i) % NH) for i in range(1, NH)],
        [near["c"]],
    ]

    def tr_copies(stage):
        return [
            pltpu.make_async_remote_copy(
                src_ref=sums.at[stage], dst_ref=got.at[stage, n], send_sem=tr_send.at[stage, n],
                recv_sem=tr_sem.at[stage, n], device_id=where, device_id_type=MESH)
            for n, where in enumerate(groups[stage])
        ]

    def tr_start(stage):
        for copy in tr_copies(stage):
            copy.start()

    def tr_finish(stage):
        total = sums[stage]
        for n, copy in enumerate(tr_copies(stage)):
            copy.wait_recv()
            total = total + got[stage, n]
        sums[stage + 1] = total

    def advance(step, _):
        tile = bbuf.at[step, bkey(0, 0)]
        for p in range(NP):
            forward("b", step, 0, 0, p, p)
        own_a = abuf.at[step, akey(0, 0), mine, :]
        other = half.at[step]
        abuf[step, akey(0, 0), mine, :] = tile[:, mine]
        half[step] = tile[:, theirs]
        for way in row_route(0, 0, 0):
            landed = asem.at[step, *landing("a", 0, 0, way), core]
            send(own_a, own_a, step, landed, near[way])
        for way in row_route(0, 0, 0):
            landed = asem.at[step, *landing("a", 0, 0, way), core]
            send(other, own_a, step, landed, near_other[way])
        send(other, own_a, step, swap_sem.at[step], near["c"])
        now = tile[...]
        halve("b", step, 0, 0, pl.ds(0, B))
        halve("a", step, 0, 0, mine)
        sums[0, pl.ds(2 * step, 1)] = fold(now * now)
        sums[0, pl.ds(2 * step + 1, 1)] = fold(now * diag)

        @pl.when(step == STEPS - 1)
        def _():
            tr_start(0)

        waiting = []
        for n, (kind, i, j, p) in enumerate(ORDER):
            arrive(place(kind, step, i, j, p), sem_of(kind, step, i, j, p), step)
            forward(kind, step, i, j, p, p)
            waiting.append((kind, i, j, p))
            for _ in range(len(waiting) if n + 1 == len(ORDER) else min(len(waiting), GAPS.get(n, 0))):
                kind, i, j, p = waiting.pop(0)
                halve(kind, step, i, j, pl.ds(p * AR, AR) if kind == "a" else pl.ds(p * BR, BR))
            if n in STAGE_AT:
                @pl.when(step == STEPS - 1)
                def _():
                    tr_finish(STAGE_AT[n])
                    tr_start(STAGE_AT[n] + 1)
        arrive(abuf.at[step, akey(0, 0), theirs, :], swap_sem.at[step], step)
        halve("a", step, 0, 0, theirs)

        def product_of(rows):
            left_hi = jnp.concatenate([ahi[k, rows, :] for k in range(NK)], axis=1)
            left_lo = jnp.concatenate([alo[k, rows, :] for k in range(NK)], axis=1)
            right_hi = jnp.concatenate([bhi[k] for k in range(NK)], axis=0)
            right_lo = jnp.concatenate([blo[k] for k in range(NK)], axis=0)
            return (jnp.dot(left_hi, right_hi, preferred_element_type=F32)
                    + jnp.dot(left_lo, right_hi, preferred_element_type=F32)
                    + jnp.dot(left_hi, right_lo, preferred_element_type=F32))

        part[step, theirs, :] = product_of(theirs)
        send(part.at[step, theirs, :], gift.at[step], step, gift_sem.at[step], near["c"])
        part[step, mine, :] = product_of(mine)
        for copy in pending[:-1]:
            copy.wait_send()
        arrive(gift.at[step], gift_sem.at[step], step)

        @pl.when(step == STEPS - 1)
        def _():
            tr_finish(3)

        product = part[step, mine, :] + gift[step]

        @pl.when(step == 0)
        def _():
            for copy in small:
                copy.wait()

        mask = [pat_ref[0, h].astype(F32) for h in range(2)]
        w = choice_ref[step].astype(F32)
        for h in range(2):
            lanes = slice(h * B, (h + 1) * B)
            new = mask[h] * ((1.0 - 2.0 * w) * product[:, lanes] + 2.0 * w * now[:, lanes])
            bbuf[step + 1, bkey(0, 0), :, lanes] = new
        pending[-1].wait_send()
        pending.clear()
        return 0

    lax.fori_loop(0, STEPS, advance, 0)
    out_ref[...] = bbuf[STEPS, bkey(0, 0)]
    for stage in range(len(groups)):
        for copy in tr_copies(stage):
            copy.wait_send()
    for step in range(STEPS):
        w = choice_ref[step].astype(F32)
        square, plain = jnp.sum(sums[4, 2 * step: 2 * step + 1]), jnp.sum(sums[4, 2 * step + 1: 2 * step + 2])
        tr_ref[step] = (1.0 - 2.0 * w) * square + 2.0 * w * plain


def shards(density, pattern, step_choices):
    smem = pl.BlockSpec(memory_space=pltpu.SMEM)
    dma = pltpu.SemaphoreType.DMA
    return pl.pallas_call(
        kernel,
        out_shape=(jax.ShapeDtypeStruct(density.shape, F32), jax.ShapeDtypeStruct((STEPS,), F32)),
        in_specs=[pl.BlockSpec(memory_space=pltpu.HBM)] * 3,
        out_specs=(pl.BlockSpec(memory_space=pltpu.VMEM), smem),
        scratch_shapes=[
            pltpu.VMEM((STEPS, NK, 2 * B, B), F32),
            pltpu.VMEM((STEPS + 1, NK, B, 2 * B), F32),
            pltpu.VMEM((STEPS, 2 * B, 2 * B), F32),
            pltpu.VMEM((STEPS, B, 2 * B), F32),
            pltpu.VMEM((5, 8, 128), F32),
            pltpu.VMEM((4, 7, 8, 128), F32),
            dma((STEPS, NZ, NL, NP)),
            dma((STEPS, NH, NX, NP)),
            dma((STEPS,)),
            dma((STEPS,)),
            dma((4, 7)),
            dma((STEPS, NSEND)),
            dma((4, 7)),
            dma((3,)),
            pltpu.VMEM((STEPS, B, B), F32),
            pltpu.SMEM((STEPS,), jnp.int32),
            pltpu.SMEM((1, 2), jnp.int32),
            *[pltpu.VMEM((NK, 2 * B, B), jnp.bfloat16)] * 2,
            *[pltpu.VMEM((NK, B, 2 * B), jnp.bfloat16)] * 2,
        ],
        compiler_params=pltpu.CompilerParams(collective_id=0, has_side_effects=True, vmem_limit_bytes=24 << 20),
    )(*(pltpu.with_memory_space_constraint(v, pltpu.HBM) for v in (step_choices, pattern, density)))


def solution(mesh):
    return jax.shard_map(
        shards,
        mesh=mesh,
        in_specs=(P("row", "col"), P("row", "col"), P()),
        out_specs=(P("row", "col"), P()),
        check_vma=False,
    )
```
